128 devices in a mesh: worker: 16 (over y_hi, x, core), fsdp: 4 (over z), tensor: 2 (over y_lo).
Axes of the slice: x: 4, y: 4 (y_hi: 2, y_lo: 2; y = y_hi * 2 + y_lo), z: 4, core: 2. Of those that a mesh axis runs over, the one named last changes fastest.
Arguments:
- normed: bfloat16 [16, 2048, 8192], P('worker', 'fsdp'), may hold values from -6 to 6
- kv_cotangent: bfloat16 [16, 2048, 2, 1024], P('worker', 'fsdp', None, 'tensor'), may hold values from -6 to 6
- local_kv: bfloat16 [16, 2, 8192, 1024], P('worker', None, 'fsdp', 'tensor'), may hold values from -0.09375 to 0.09375
- global_kv: float32 [2, 4, 2048, 1024], P(None, 'fsdp', 'worker', 'tensor'), may hold values from -0.0625 to 0.0625
- momentum: float32 [2, 4, 2048, 1024], P(None, 'fsdp', 'worker', 'tensor'), may hold values from -0.0625 to 0.0625
Outputs:
- new_global: float32 [2, 4, 2048, 1024], P(None, 'fsdp', 'worker', 'tensor')
- new_momentum: float32 [2, 4, 2048, 1024], P(None, 'fsdp', 'worker', 'tensor')
- keys_values: bfloat16 [16, 2048, 2, 1024], P('worker', 'fsdp', None, 'tensor')
- kv_grad: bfloat16 [16, 2, 8192, 1024], P('worker', None, 'fsdp', 'tensor')
- normed_grad: bfloat16 [16, 2048, 8192], P('worker', 'fsdp', 'tensor')
The draws below stay inside these ranges and needn't reach their ends.
All inputs are finite; a program needn't handle non-finite values.
Results may differ from the reference program's by a relative error of at most 0.019.
Values may be sent and summed in bfloat16 or wider, within the bound.
A program may use at most 192 MiB of HBM per device.

```python
import math
import jax
import jax.numpy as jnp
from jax import lax

D = 8192
KV_HEADS = 8
HEAD_DIM = 128
TOK_DEV = 512
KVC = 1024
SEQ = 2048
N_WORKER = 16
N_FSDP = 4
N_TENSOR = 2


def strengthened(entries, own_key, source, target, parts, factor):
    owner, partner = [(jnp.arange(entries.shape[dim]) // (entries.shape[dim] // parts)).reshape([-1 if axis == dim else 1 for axis in range(entries.ndim)]) for dim in (source, target)]
    chosen = jax.random.permutation(own_key, parts)[partner]
    strong = (owner == chosen) | (owner == (partner + parts // 2) % parts)
    return jnp.where(strong, factor * entries, entries)


def levels(key, extent, pieces, smallest, largest):
    level, own = 1.0, jax.random.fold_in(key, 6)
    for position, shards_of in pieces:
        steps = jnp.exp(jax.random.uniform(jax.random.fold_in(own, position), (shards_of,), jnp.float32, smallest / len(pieces), largest / len(pieces)))
        level = level * jnp.repeat(steps, extent[position] // shards_of).reshape([-1 if axis == position else 1 for axis in range(len(extent))])
    return level


def gaussian(own_key, shape, width, bound, shards=(), kind=jnp.bfloat16):
    entries = jax.random.normal(own_key, shape, jnp.float32) * width
    if len(shards) > 0:
        entries = levels(own_key, shape, shards, -0.22, 0.18) * entries
    return jnp.clip(entries, min=-bound, max=bound).astype(kind)


def noise_with(rng, shape, deviation, most, shards, heavy, kind=jnp.bfloat16):
    entries = deviation * jax.random.normal(rng, shape, jnp.float32)
    if shards:
        entries = entries * levels(rng, shape, shards, -0.22, 0.18)
    return jnp.clip(strengthened(entries, jax.random.fold_in(rng, 3), *heavy), -most, most).astype(kind)


def setup_inputs(seed: int = 0) -> dict:
    key_of = jax.random.split(jax.random.key(seed), 6)
    return {
        "normed": gaussian(key_of[0], (N_WORKER, SEQ, D), 1.0, 6.0, ((0, 16), (1, 4))),
        "kv_cotangent": gaussian(key_of[1], (N_WORKER, SEQ, 2, KVC), 1.0, 6.0, ((0, 16), (1, 4), (3, 2))),
        "local_kv": noise_with(key_of[2], (N_WORKER, 2, D, KVC), D ** -0.5, 0.09375, ((0, 16), (2, 4), (3, 2)), (0, 2, 16, 2.0)),
        "global_kv": gaussian(key_of[3], (2, N_FSDP, D // N_FSDP, KVC), D ** -0.5, 0.0625, ((1, 4), (2, 16), (3, 2)), jnp.float32),
        "momentum": gaussian(key_of[4], (2, N_FSDP, D // N_FSDP, KVC), D ** -0.5, 0.0625, ((1, 4), (2, 16), (3, 2)), jnp.float32),
    }


def rotate(block, pos, sign):
    half = block.shape[-1] // 2
    index = jnp.arange(half, dtype=jnp.float32)
    freq = jnp.exp(-(2.0 * index / block.shape[-1]) * math.log(500000.0))
    angle = pos[:, None] * freq[None, :]
    cosine = jnp.cos(angle)[:, None, :]
    sine = jnp.sin(angle)[:, None, :]
    first = block[..., :half]
    second = block[..., half:]
    return jnp.concatenate([first * cosine - sign * second * sine, second * cosine + sign * first * sine], axis=-1)


def reference(normed, kv_cotangent, local_kv, global_kv, momentum):
    def accumulate(total, piece):
        return total + piece.astype(jnp.float32), None

    summed, _ = lax.scan(accumulate, jnp.zeros((2, D, KVC), jnp.float32), local_kv)
    old = global_kv.reshape(2, D, KVC)
    pseudo = old - summed / N_WORKER
    new_mom = 0.9 * momentum.reshape(2, D, KVC) + pseudo
    new_glob = old - 0.7 * (pseudo + 0.9 * new_mom)
    weights = new_glob.astype(jnp.bfloat16)
    weights_wide = weights.astype(jnp.float32)
    pos = jnp.arange(SEQ).astype(jnp.float32)

    def replica(pair):
        tokens, cotangent = pair
        tokens_wide = tokens.astype(jnp.float32)
        proj = jnp.einsum("sr,trc->stc", tokens_wide, weights_wide, preferred_element_type=jnp.float32)
        keys = rotate(proj[:, 0].reshape(SEQ, KV_HEADS, HEAD_DIM), pos, 1.0).reshape(SEQ, KVC)
        kv_out = jnp.stack([keys, proj[:, 1]], axis=1).astype(jnp.bfloat16)
        cot_wide = cotangent.astype(jnp.float32)
        back = rotate(cot_wide[:, 0].reshape(SEQ, KV_HEADS, HEAD_DIM), pos, -1.0).reshape(SEQ, KVC)
        raw = jnp.stack([back, cot_wide[:, 1]], axis=1).astype(jnp.bfloat16)
        raw_wide = raw.astype(jnp.float32)
        blocks_in = tokens_wide.reshape(N_FSDP, TOK_DEV, D)
        blocks_cot = raw_wide.reshape(N_FSDP, TOK_DEV, 2, KVC)

        def block_term(total, piece):
            term = jnp.einsum("sr,stc->trc", piece[0], piece[1], preferred_element_type=jnp.float32)
            term = lax.optimization_barrier(term.astype(jnp.bfloat16))
            return total + term.astype(jnp.float32), None

        grad, _ = lax.scan(block_term, jnp.zeros((2, D, KVC), jnp.float32), (blocks_in, blocks_cot))
        halves = jnp.einsum("sthc,trhc->hsr", raw_wide.reshape(SEQ, 2, N_TENSOR, KVC // N_TENSOR),
                            weights_wide.reshape(2, D, N_TENSOR, KVC // N_TENSOR), preferred_element_type=jnp.float32)
        halves = lax.optimization_barrier(halves.astype(jnp.bfloat16))
        dnormed = jnp.sum(halves.astype(jnp.float32), axis=0)
        return kv_out, grad.astype(jnp.bfloat16), dnormed.astype(jnp.bfloat16)

    kv_all, grad_all, dnormed_all = lax.map(replica, (normed, kv_cotangent))
    shape = (2, N_FSDP, D // N_FSDP, KVC)
    return new_glob.reshape(shape), new_mom.reshape(shape), kv_all, grad_all, dnormed_all
```

```python
import math

import jax
import jax.numpy as jnp
from jax import lax
from jax.sharding import PartitionSpec as P

HEAD_DIM = 128


def rotate(block, pos, sign):
    half = block.shape[-1] // 2
    index = jnp.arange(half, dtype=jnp.float32)
    freq = jnp.exp(-(2.0 * index / block.shape[-1]) * math.log(500000.0))
    angle = pos[:, None] * freq[None, :]
    cosine = jnp.cos(angle)[:, None, :]
    sine = jnp.sin(angle)[:, None, :]
    first = block[..., :half]
    second = block[..., half:]
    return jnp.concatenate(
        [first * cosine - sign * second * sine, second * cosine + sign * first * sine], axis=-1
    )


CORES, ALONG_X = 2, 4


def move_core():
    return [(w, w ^ 1) for w in range(16)]


def move_y():
    return [(w, w ^ 8) for w in range(16)]


def move_x(d):
    return [(w, (w & 9) | ((((w >> 1) + d) & 3) << 1)) for w in range(16)]


def after(value, *earlier):
    return lax.optimization_barrier((value, *earlier))[0]


def take(array, index, axis):
    return lax.dynamic_index_in_dim(array, index, axis, keepdims=False)


def per_device(normed, kv_cotangent, local_kv, global_kv, momentum):
    replicas = lax.axis_size("worker")
    n_fsdp = lax.axis_size("fsdp")
    worker = lax.axis_index("worker")
    core, here, upper = worker & 1, (worker >> 1) & 3, worker >> 3
    me = lax.axis_index("fsdp")
    side = lax.axis_index("tensor")
    tokens = normed[0]
    count, width = tokens.shape
    rows = width // n_fsdp
    columns = local_kv.shape[3]
    heads = columns // HEAD_DIM
    shard = global_kv.shape[2]
    f32, bf16 = jnp.float32, jnp.bfloat16

    local = local_kv[0].reshape(2, 2, ALONG_X, CORES, shard, columns)
    got = lax.ppermute(take(local, 1 - core, 3), "worker", move_core())

    pos = (me * count + jnp.arange(count)).astype(f32)
    cotangent = kv_cotangent[0]
    back = rotate(
        cotangent[:, 0].astype(f32).reshape(count, heads, HEAD_DIM), pos, -1.0
    ).reshape(count, columns)
    raw = (back.astype(bf16), cotangent[:, 1])

    def ring(step, running):
        ready = []
        for kind, way in ((0, 1), (1, -1)):
            block = (me - way * (step + 1)) & (n_fsdp - 1)
            part = lax.dynamic_slice_in_dim(tokens, block * rows, rows, axis=1)
            mine = jnp.einsum("sr,sc->rc", part, raw[kind], preferred_element_type=f32)
            if step > 0:
                mine = mine + running[kind].astype(f32)
            ready.append(mine.astype(bf16))
        if step == n_fsdp - 1:
            return ready
        return [
            lax.ppermute(out, "fsdp", [(a, (a + way) % n_fsdp) for a in range(n_fsdp)])
            for out, way in zip(ready, (1, -1))
        ]

    pair = (take(local, core, 3).astype(f32) + got.astype(f32)).astype(bf16)
    arrived = [
        lax.ppermute(take(pair, (here + d) & 3, 2), "worker", move_x(d)) for d in (1, 3, 2)
    ]
    running = ring(0, None)
    total = take(pair, here, 2).astype(f32)
    for piece in arrived:
        total = total + piece.astype(f32)
    total = total.astype(bf16)
    got = lax.ppermute(take(total, 1 - upper, 1), "worker", move_y())
    summed = take(total, upper, 1).astype(f32) + got.astype(f32)

    old = global_kv[:, 0]
    pseudo = old - summed / replicas
    new_mom = 0.9 * momentum[:, 0] + pseudo
    new_glob = old - 0.7 * (pseudo + 0.9 * new_mom)
    fresh = new_glob.astype(bf16)
    pieces = [fresh] + [
        lax.ppermute(fresh, "fsdp", [(a, (a + d) % n_fsdp) for a in range(n_fsdp)])
        for d in (1, 2, 3)
    ]
    four = jnp.stack(
        [lax.select_n((me - f) & (n_fsdp - 1), *pieces) for f in range(n_fsdp)], axis=1
    )
    across = lax.ppermute(four, "worker", move_y())
    running = ring(1, [after(r, four) for r in running])
    block = jnp.stack(
        [jnp.where(upper == 0, four, across), jnp.where(upper == 0, across, four)], axis=2
    )
    blocks = [block] + [lax.ppermute(block, "worker", move_x(d)) for d in (1, 3, 2)]
    group = 2 * n_fsdp

    def head(chunk, which):
        part = lax.dynamic_slice_in_dim(chunk, which * (n_fsdp // 2), n_fsdp // 2, axis=1)
        part = part.reshape(2, group // 2 * shard, columns)
        first = jnp.einsum("sc,rc->sr", raw[0], part[0], preferred_element_type=f32)
        return first + jnp.einsum("sc,rc->sr", raw[1], part[1], preferred_element_type=f32)

    def weave(own, other):
        own, other = [a.reshape(count, group // 2, shard) for a in (own, other)]
        low, high = jnp.where(core == 0, own, other), jnp.where(core == 0, other, own)
        return jnp.concatenate(
            [a[:, g] for g in range(group // 2) for a in (low, high)], axis=1
        )

    proj = jnp.zeros((2, count, columns), f32)
    dn = []
    last = None
    for n, d in enumerate((0, 1, 3, 2)):
        mine = blocks[n]
        other = lax.ppermute(mine, "worker", move_core())
        sent = weave(head(mine, 1 - side).astype(bf16), head(other, 1 - side).astype(bf16))
        theirs = lax.ppermute(sent, "tensor", [(0, 1), (1, 0)])
        if n == 1:
            running = ring(2, [after(r, last) for r in running])
        kept = weave(head(mine, side).astype(bf16), head(other, side).astype(bf16))
        dn.append((kept.astype(f32) + theirs.astype(f32)).astype(bf16))
        place = (here - d) & 3
        for which, chunk in ((core, mine), (1 - core, other)):
            part = jnp.concatenate(
                [
                    lax.dynamic_slice_in_dim(
                        tokens, g * 8 * shard + (place * CORES + which) * shard, shard, axis=1
                    )
                    for g in range(group)
                ],
                axis=1,
            )
            proj = proj + jnp.einsum(
                "sr,trc->tsc",
                part,
                chunk.reshape(2, group * shard, columns),
                preferred_element_type=f32,
            )
        last = sent
    grad = jnp.stack(ring(3, running))
    keys = rotate(proj[0].reshape(count, heads, HEAD_DIM), pos, 1.0).reshape(count, columns)
    kv_out = jnp.stack([keys, proj[1]], axis=1).astype(bf16)
    order = [dn[0], dn[1], dn[3], dn[2]]
    wide = CORES * shard
    placed = [lax.select_n((here - x) & 3, *order) for x in range(ALONG_X)]
    dnormed = jnp.concatenate(
        [
            placed[x][:, g * wide : (g + 1) * wide]
            for g in range(group // 2)
            for x in range(ALONG_X)
        ],
        axis=1,
    )
    return (new_glob[:, None], new_mom[:, None], kv_out[None], grad[None], dnormed[None])


def solution(mesh):
    placed = (
        P("worker", "fsdp", None),
        P("worker", "fsdp", None, "tensor"),
        P("worker", None, "fsdp", "tensor"),
        P(None, "fsdp", "worker", "tensor"),
        P(None, "fsdp", "worker", "tensor"),
    )
    return jax.shard_map(
        per_device,
        mesh=mesh,
        in_specs=placed,
        out_specs=(
            P(None, "fsdp", "worker", "tensor"),
            P(None, "fsdp", "worker", "tensor"),
            P("worker", "fsdp", None, "tensor"),
            P("worker", None, "fsdp", "tensor"),
            P("worker", "fsdp", "tensor"),
        ),
        check_vma=False,
    )
```

```python
import math

import jax
import jax.numpy as jnp
from jax import lax
from jax.experimental import pallas as pl
from jax.experimental.pallas import tpu as pltpu
from jax.sharding import PartitionSpec as P

HEAD_DIM = 128


def rotate(block, pos, sign):
    half = block.shape[-1] // 2
    index = jnp.arange(half, dtype=jnp.float32)
    freq = jnp.exp(-(2.0 * index / block.shape[-1]) * math.log(500000.0))
    angle = pos[:, None] * freq[None, :]
    cosine = jnp.cos(angle)[:, None, :]
    sine = jnp.sin(angle)[:, None, :]
    first = block[..., :half]
    second = block[..., half:]
    return jnp.concatenate(
        [first * cosine - sign * second * sine, second * cosine + sign * first * sine], axis=-1
    )


def put_kernel(slots, kept, theirs, *rest):
    rest[-1][...] = (kept[0].astype(jnp.float32) + theirs[0].astype(jnp.float32)).astype(
        rest[-1].dtype
    )


def put(slots, kept, theirs, wide, width):
    cores, count, length = kept.shape
    lane = 128
    piece = pl.BlockSpec((1, count, lane), lambda k, g, slots: (k, 0, g))
    earlier = () if wide is None else (wide,)
    return pl.pallas_call(
        put_kernel,
        out_shape=jax.ShapeDtypeStruct((count, width), kept.dtype),
        grid_spec=pltpu.PrefetchScalarGridSpec(
            num_scalar_prefetch=1,
            grid=(cores, length // lane),
            in_specs=[piece, piece] + [pl.BlockSpec(memory_space=pl.ANY)] * len(earlier),
            out_specs=pl.BlockSpec((count, lane), lambda k, g, slots: (0, g * 8 + slots[k])),
        ),
        input_output_aliases={3: 0} if earlier else {},
        cost_estimate=pl.CostEstimate(
            flops=kept.size, bytes_accessed=6 * kept.size, transcendentals=0
        ),
    )(slots, kept, theirs, *earlier)


CORES, ALONG_X = 2, 4


def move_core():
    return [(w, w ^ 1) for w in range(16)]


def move_y():
    return [(w, w ^ 8) for w in range(16)]


def move_x(d):
    return [(w, (w & 9) | ((((w >> 1) + d) & 3) << 1)) for w in range(16)]


def after(value, *earlier):
    return lax.optimization_barrier((value, *earlier))[0]


def take(array, index, axis):
    return lax.dynamic_index_in_dim(array, index, axis, keepdims=False)


def per_device(normed, kv_cotangent, local_kv, global_kv, momentum):
    replicas = lax.axis_size("worker")
    n_fsdp = lax.axis_size("fsdp")
    worker = lax.axis_index("worker")
    core, here, upper = worker & 1, (worker >> 1) & 3, worker >> 3
    me = lax.axis_index("fsdp")
    side = lax.axis_index("tensor")
    tokens = normed[0]
    count, width = tokens.shape
    rows = width // n_fsdp
    columns = local_kv.shape[3]
    heads = columns // HEAD_DIM
    shard = global_kv.shape[2]
    f32, bf16 = jnp.float32, jnp.bfloat16

    local = local_kv[0].reshape(2, 2, ALONG_X, CORES, shard, columns)
    got = lax.ppermute(take(local, 1 - core, 3), "worker", move_core())

    pos = (me * count + jnp.arange(count)).astype(f32)
    cotangent = kv_cotangent[0]
    back = rotate(
        cotangent[:, 0].astype(f32).reshape(count, heads, HEAD_DIM), pos, -1.0
    ).reshape(count, columns)
    raw = (back.astype(bf16), cotangent[:, 1])
    both = jnp.concatenate(raw, axis=1)

    def ring(step, running):
        ready = []
        for kind, way in ((0, 1), (1, -1)):
            block = (me - way * (step + 1)) & (n_fsdp - 1)
            part = lax.dynamic_slice_in_dim(tokens, block * rows, rows, axis=1)
            mine = jnp.einsum("sr,sc->rc", part, raw[kind], preferred_element_type=f32)
            if step > 0:
                mine = mine + running[kind].astype(f32)
            ready.append(mine.astype(bf16))
        if step == n_fsdp - 1:
            return ready, ready
        moved = [
            lax.ppermute(out, "fsdp", [(a, (a + way) % n_fsdp) for a in range(n_fsdp)])
            for out, way in zip(ready, (1, -1))
        ]
        return ready, moved

    pair = (take(local, core, 3).astype(f32) + got.astype(f32)).astype(bf16)
    ready, running = ring(0, None)
    pair = after(pair, *ready)
    arrived = [
        lax.ppermute(take(pair, (here + d) & 3, 2), "worker", move_x(d)) for d in (1, 3, 2)
    ]
    total = take(pair, here, 2).astype(f32)
    for piece in arrived:
        total = total + piece.astype(f32)
    total = total.astype(bf16)
    got = lax.ppermute(take(total, 1 - upper, 1), "worker", move_y())
    summed = take(total, upper, 1).astype(f32) + got.astype(f32)

    old = global_kv[:, 0]
    pseudo = old - summed / replicas
    new_mom = 0.9 * momentum[:, 0] + pseudo
    new_glob = old - 0.7 * (pseudo + 0.9 * new_mom)
    fresh = jnp.concatenate([new_glob[0], new_glob[1]], axis=1).astype(bf16)
    pieces = [fresh] + [
        lax.ppermute(fresh, "fsdp", [(a, (a + d) % n_fsdp) for a in range(n_fsdp)])
        for d in (1, 2, 3)
    ]
    four = jnp.stack([lax.select_n((me - f) & (n_fsdp - 1), *pieces) for f in range(n_fsdp)])
    across = lax.ppermute(four, "worker", move_y())
    block = jnp.stack(
        [jnp.where(upper == 0, four, across), jnp.where(upper == 0, across, four)], axis=1
    )
    group = 2 * n_fsdp
    block = block.reshape(group * shard, 2 * columns)
    ready, running = ring(1, [after(r, four) for r in running])
    blocks = [block] + [lax.ppermute(block, "worker", move_x(d)) for d in (1, 3, 2)]
    half = group * shard // 2

    def head(chunk):
        found = jnp.einsum("sk,rk->sr", both, chunk, preferred_element_type=f32).astype(bf16)
        low, high = found[:, :half], found[:, half:]
        return jnp.where(side == 0, low, high), jnp.where(side == 0, high, low)

    proj = None
    dnormed = None
    for n, d in enumerate((0, 1, 3, 2)):
        mine = blocks[n]
        if n == 1 or n == 3:
            mine = after(mine, *ready)
        other = lax.ppermute(mine, "worker", move_core())
        kept_mine, sent_mine = head(mine)
        kept_other, sent_other = head(other)
        sent = jnp.stack([sent_mine, sent_other])
        theirs = lax.ppermute(sent, "tensor", [(0, 1), (1, 0)])
        if n == 2:
            ready, running = ring(2, [after(r, sent) for r in running])
        kept = jnp.stack([kept_mine, kept_other])
        place = (here - d) & 3
        for which, chunk in ((core, mine), (1 - core, other)):
            part = jnp.concatenate(
                [
                    lax.dynamic_slice_in_dim(
                        tokens, g * 8 * shard + (place * CORES + which) * shard, shard, axis=1
                    )
                    for g in range(group)
                ],
                axis=1,
            )
            more = jnp.dot(part, chunk, preferred_element_type=f32)
            proj = more if proj is None else proj + more
        slots = jnp.stack([place * CORES + core, place * CORES + 1 - core])
        dnormed = put(slots, kept, theirs, dnormed, width // 2)
    grad = jnp.stack(ring(3, [after(r, sent) for r in running])[0])
    keys = rotate(
        proj[:, :columns].reshape(count, heads, HEAD_DIM), pos, 1.0
    ).reshape(count, columns)
    kv_out = jnp.stack([keys, proj[:, columns:]], axis=1).astype(bf16)
    return (new_glob[:, None], new_mom[:, None], kv_out[None], grad[None], dnormed[None])


def solution(mesh):
    placed = (
        P("worker", "fsdp", None),
        P("worker", "fsdp", None, "tensor"),
        P("worker", None, "fsdp", "tensor"),
        P(None, "fsdp", "worker", "tensor"),
        P(None, "fsdp", "worker", "tensor"),
    )
    return jax.shard_map(
        per_device,
        mesh=mesh,
        in_specs=placed,
        out_specs=(
            P(None, "fsdp", "worker", "tensor"),
            P(None, "fsdp", "worker", "tensor"),
            P("worker", "fsdp", None, "tensor"),
            P("worker", None, "fsdp", "tensor"),
            P("worker", "fsdp", "tensor"),
        ),
        check_vma=False,
    )
```

```python
import math

import jax
import jax.numpy as jnp
from jax import lax
from jax.experimental import pallas as pl
from jax.experimental.pallas import tpu as pltpu
from jax.sharding import PartitionSpec as P

HEAD_DIM = 128


def rotate(block, pos, sign):
    half = block.shape[-1] // 2
    index = jnp.arange(half, dtype=jnp.float32)
    freq = jnp.exp(-(2.0 * index / block.shape[-1]) * math.log(500000.0))
    angle = pos[:, None] * freq[None, :]
    cosine = jnp.cos(angle)[:, None, :]
    sine = jnp.sin(angle)[:, None, :]
    first = block[..., :half]
    second = block[..., half:]
    return jnp.concatenate(
        [first * cosine - sign * second * sine, second * cosine + sign * first * sine], axis=-1
    )


def put_kernel(slots, kept, theirs, *rest):
    rest[-1][...] = (kept[0].astype(jnp.float32) + theirs[0].astype(jnp.float32)).astype(
        rest[-1].dtype
    )


def put(slots, kept, theirs, wide, width):
    cores, count, length = kept.shape
    lane = 128
    piece = pl.BlockSpec((1, count, lane), lambda k, g, slots: (k, 0, g))
    earlier = () if wide is None else (wide,)
    return pl.pallas_call(
        put_kernel,
        out_shape=jax.ShapeDtypeStruct((count, width), kept.dtype),
        grid_spec=pltpu.PrefetchScalarGridSpec(
            num_scalar_prefetch=1,
            grid=(cores, length // lane),
            in_specs=[piece, piece] + [pl.BlockSpec(memory_space=pl.ANY)] * len(earlier),
            out_specs=pl.BlockSpec((count, lane), lambda k, g, slots: (0, g * 8 + slots[k])),
        ),
        input_output_aliases={3: 0} if earlier else {},
        cost_estimate=pl.CostEstimate(
            flops=kept.size, bytes_accessed=6 * kept.size, transcendentals=0
        ),
    )(slots, kept, theirs, *earlier)


CORES, ALONG_X = 2, 4


def move_core():
    return [(w, w ^ 1) for w in range(16)]


def move_y():
    return [(w, w ^ 8) for w in range(16)]


def move_x(d):
    return [(w, (w & 9) | ((((w >> 1) + d) & 3) << 1)) for w in range(16)]


def after(value, *earlier):
    return lax.optimization_barrier((value, *earlier))[0]


def take(array, index, axis):
    return lax.dynamic_index_in_dim(array, index, axis, keepdims=False)


def per_device(normed, kv_cotangent, local_kv, global_kv, momentum):
    replicas = lax.axis_size("worker")
    n_fsdp = lax.axis_size("fsdp")
    worker = lax.axis_index("worker")
    core, here, upper = worker & 1, (worker >> 1) & 3, worker >> 3
    me = lax.axis_index("fsdp")
    side = lax.axis_index("tensor")
    tokens = normed[0]
    count, width = tokens.shape
    rows = width // n_fsdp
    columns = local_kv.shape[3]
    heads = columns // HEAD_DIM
    shard = global_kv.shape[2]
    f32, bf16 = jnp.float32, jnp.bfloat16

    local = local_kv[0].reshape(2, 2, ALONG_X, CORES, shard, columns)
    got = lax.ppermute(take(local, 1 - core, 3), "worker", move_core())

    pos = (me * count + jnp.arange(count)).astype(f32)
    cotangent = kv_cotangent[0]
    back = rotate(
        cotangent[:, 0].astype(f32).reshape(count, heads, HEAD_DIM), pos, -1.0
    ).reshape(count, columns)
    raw = (back.astype(bf16), cotangent[:, 1])
    both = jnp.concatenate(raw, axis=1)

    def ring(step, running, tokens):
        ready = []
        for kind, way in ((0, 1), (1, -1)):
            block = (me - way * (step + 1)) & (n_fsdp - 1)
            part = lax.dynamic_slice_in_dim(tokens, block * rows, rows, axis=1)
            mine = jnp.einsum("sr,sc->rc", part, raw[kind], preferred_element_type=f32)
            if step > 0:
                mine = mine + running[kind].astype(f32)
            ready.append(mine.astype(bf16))
        if step == n_fsdp - 1:
            return ready, ready
        moved = [
            lax.ppermute(out, "fsdp", [(a, (a + way) % n_fsdp) for a in range(n_fsdp)])
            for out, way in zip(ready, (1, -1))
        ]
        return ready, moved

    pair = (take(local, core, 3).astype(f32) + got.astype(f32)).astype(bf16)
    arrived = [
        lax.ppermute(take(pair, (here + d) & 3, 2), "worker", move_x(d)) for d in (1, 3, 2)
    ]
    ready, running = ring(0, None, after(tokens, pair))
    total = after(take(pair, here, 2), *ready).astype(f32)
    for piece in arrived:
        total = total + piece.astype(f32)
    total = total.astype(bf16)
    got = lax.ppermute(take(total, 1 - upper, 1), "worker", move_y())
    summed = take(total, upper, 1).astype(f32) + got.astype(f32)

    old = global_kv[:, 0]
    pseudo = old - summed / replicas
    new_mom = 0.9 * momentum[:, 0] + pseudo
    new_glob = old - 0.7 * (pseudo + 0.9 * new_mom)
    fresh = jnp.concatenate([new_glob[0], new_glob[1]], axis=1).astype(bf16)
    pieces = [fresh] + [
        lax.ppermute(fresh, "fsdp", [(a, (a + d) % n_fsdp) for a in range(n_fsdp)])
        for d in (1, 2, 3)
    ]
    four = jnp.stack([lax.select_n((me - f) & (n_fsdp - 1), *pieces) for f in range(n_fsdp)])
    across = lax.ppermute(four, "worker", move_y())
    block = jnp.stack(
        [jnp.where(upper == 0, four, across), jnp.where(upper == 0, across, four)], axis=1
    )
    group = 2 * n_fsdp
    block = block.reshape(group * shard, 2 * columns)
    ready, running = ring(1, [after(r, four) for r in running], after(tokens, fresh))
    left = lax.ppermute(block, "worker", move_x(1))
    right = lax.ppermute(block, "worker", move_x(3))
    late = after(tokens, four)
    half = group * shard // 2

    def head(chunk):
        found = jnp.einsum("sk,rk->sr", both, chunk, preferred_element_type=f32).astype(bf16)
        low, high = found[:, :half], found[:, half:]
        return jnp.where(side == 0, low, high), jnp.where(side == 0, high, low)

    def spread(chunk):
        other = lax.ppermute(chunk, "worker", move_core())
        pairs = [head(chunk), head(other)]
        return other, [p[0] for p in pairs], [p[1] for p in pairs]

    def project(total, d, mine, other):
        place = (here - d) & 3
        for which, chunk in ((core, mine), (1 - core, other)):
            part = jnp.concatenate(
                [
                    lax.dynamic_slice_in_dim(
                        late, g * 8 * shard + (place * CORES + which) * shard, shard, axis=1
                    )
                    for g in range(group)
                ],
                axis=1,
            )
            more = jnp.dot(part, chunk, preferred_element_type=f32)
            total = more if total is None else total + more
        return total

    def slots(*hops):
        places = [((here - d) & 3) * CORES for d in hops]
        return jnp.stack([s for p in places for s in (p + core, p + 1 - core)])

    swap = [(0, 1), (1, 0)]
    other, kept0, sent = spread(block)
    sent = jnp.stack(sent)
    theirs0 = lax.ppermute(sent, "tensor", swap)
    proj = project(None, 0, block, other)
    left, right = after(left, sent, *ready), after(right, sent, *ready)
    up = lax.ppermute(left[:half], "worker", move_x(1))
    down = lax.ppermute(right[half:], "worker", move_x(3))
    other_left, kept1, sent_left = spread(left)
    other_right, kept3, sent_right = spread(right)
    sent = jnp.stack(sent_left + sent_right)
    theirs1 = lax.ppermute(sent, "tensor", swap)
    ready, running = ring(2, [after(r, sent) for r in running], late)
    far = jnp.concatenate([after(up, *ready), down], axis=0)
    proj = project(proj, 1, left, other_left)
    proj = project(proj, 3, right, other_right)
    other, kept2, sent = spread(far)
    sent = jnp.stack(sent)
    theirs2 = lax.ppermute(sent, "tensor", swap)
    proj = project(proj, 2, far, other)
    near = after(jnp.stack(kept0), sent)
    dnormed = put(slots(0), near, after(theirs0, sent), None, width // 2)
    near = after(jnp.stack(kept1 + kept3), sent)
    dnormed = put(slots(1, 3), near, after(theirs1, sent), dnormed, width // 2)
    dnormed = put(slots(2), jnp.stack(kept2), theirs2, dnormed, width // 2)
    grad = jnp.stack(ring(3, [after(r, sent) for r in running], late)[0])
    keys = rotate(
        proj[:, :columns].reshape(count, heads, HEAD_DIM), pos, 1.0
    ).reshape(count, columns)
    kv_out = jnp.stack([keys, proj[:, columns:]], axis=1).astype(bf16)
    return (new_glob[:, None], new_mom[:, None], kv_out[None], grad[None], dnormed[None])


def solution(mesh):
    placed = (
        P("worker", "fsdp", None),
        P("worker", "fsdp", None, "tensor"),
        P("worker", None, "fsdp", "tensor"),
        P(None, "fsdp", "worker", "tensor"),
        P(None, "fsdp", "worker", "tensor"),
    )
    return jax.shard_map(
        per_device,
        mesh=mesh,
        in_specs=placed,
        out_specs=(
            P(None, "fsdp", "worker", "tensor"),
            P(None, "fsdp", "worker", "tensor"),
            P("worker", "fsdp", None, "tensor"),
            P("worker", None, "fsdp", "tensor"),
            P("worker", "fsdp", "tensor"),
        ),
        check_vma=False,
    )
```

```python
import math

import jax
import jax.numpy as jnp
from jax import lax
from jax.experimental import pallas as pl
from jax.experimental.pallas import tpu as pltpu
from jax.sharding import PartitionSpec as P

HEAD_DIM = 128


def rotate(block, pos, sign):
    half = block.shape[-1] // 2
    index = jnp.arange(half, dtype=jnp.float32)
    freq = jnp.exp(-(2.0 * index / block.shape[-1]) * math.log(500000.0))
    angle = pos[:, None] * freq[None, :]
    cosine = jnp.cos(angle)[:, None, :]
    sine = jnp.sin(angle)[:, None, :]
    first = block[..., :half]
    second = block[..., half:]
    return jnp.concatenate(
        [first * cosine - sign * second * sine, second * cosine + sign * first * sine], axis=-1
    )


def put_kernel(slots, kept, theirs, *rest):
    rest[-1][...] = (kept[0].astype(jnp.float32) + theirs[0].astype(jnp.float32)).astype(
        rest[-1].dtype
    )


def put(slots, kept, theirs, wide, width):
    cores, count, length = kept.shape
    lane = 128
    piece = pl.BlockSpec((1, count, lane), lambda k, g, slots: (k, 0, g))
    earlier = () if wide is None else (wide,)
    return pl.pallas_call(
        put_kernel,
        out_shape=jax.ShapeDtypeStruct((count, width), kept.dtype),
        grid_spec=pltpu.PrefetchScalarGridSpec(
            num_scalar_prefetch=1,
            grid=(cores, length // lane),
            in_specs=[piece, piece] + [pl.BlockSpec(memory_space=pl.ANY)] * len(earlier),
            out_specs=pl.BlockSpec((count, lane), lambda k, g, slots: (0, g * 8 + slots[k])),
        ),
        input_output_aliases={3: 0} if earlier else {},
        cost_estimate=pl.CostEstimate(
            flops=kept.size, bytes_accessed=6 * kept.size, transcendentals=0
        ),
    )(slots, kept, theirs, *earlier)


CORES, ALONG_X = 2, 4


def move_core():
    return [(w, w ^ 1) for w in range(16)]


def move_y():
    return [(w, w ^ 8) for w in range(16)]


def move_x(d):
    return [(w, (w & 9) | ((((w >> 1) + d) & 3) << 1)) for w in range(16)]


def after(value, *earlier):
    return lax.optimization_barrier((value, *earlier))[0]


def take(array, index, axis):
    return lax.dynamic_index_in_dim(array, index, axis, keepdims=False)


def per_device(normed, kv_cotangent, local_kv, global_kv, momentum):
    replicas = lax.axis_size("worker")
    n_fsdp = lax.axis_size("fsdp")
    worker = lax.axis_index("worker")
    core, here, upper = worker & 1, (worker >> 1) & 3, worker >> 3
    me = lax.axis_index("fsdp")
    side = lax.axis_index("tensor")
    tokens = normed[0]
    count, width = tokens.shape
    rows = width // n_fsdp
    columns = local_kv.shape[3]
    heads = columns // HEAD_DIM
    shard = global_kv.shape[2]
    f32, bf16 = jnp.float32, jnp.bfloat16

    local = local_kv[0].reshape(2, 2, ALONG_X, CORES, shard, columns)
    got = lax.ppermute(take(local, 1 - core, 3), "worker", move_core())

    pos = (me * count + jnp.arange(count)).astype(f32)
    cotangent = kv_cotangent[0]
    back = rotate(
        cotangent[:, 0].astype(f32).reshape(count, heads, HEAD_DIM), pos, -1.0
    ).reshape(count, columns)
    raw = (back.astype(bf16), cotangent[:, 1])
    both = jnp.concatenate(raw, axis=1)

    def ring_terms(step, running, tokens):
        ready = []
        for kind, way in ((0, 1), (1, -1)):
            block = (me - way * (step + 1)) & (n_fsdp - 1)
            part = lax.dynamic_slice_in_dim(tokens, block * rows, rows, axis=1)
            mine = jnp.einsum("sr,sc->rc", part, raw[kind], preferred_element_type=f32)
            if step > 0:
                mine = mine + running[kind].astype(f32)
            ready.append(mine.astype(bf16))
        return ready

    def ring_move(ready):
        return [
            lax.ppermute(out, "fsdp", [(a, (a + way) % n_fsdp) for a in range(n_fsdp)])
            for out, way in zip(ready, (1, -1))
        ]

    pair = (take(local, core, 3).astype(f32) + got.astype(f32)).astype(bf16)
    arrived = [
        lax.ppermute(take(pair, (here + d) & 3, 2), "worker", move_x(d)) for d in (1, 3, 2)
    ]
    ready = ring_terms(0, None, after(tokens, pair))
    total = after(take(pair, here, 2), *ready).astype(f32)
    for piece in arrived:
        total = total + piece.astype(f32)
    total = total.astype(bf16)
    got = lax.ppermute(take(total, 1 - upper, 1), "worker", move_y())
    summed = take(total, upper, 1).astype(f32) + got.astype(f32)

    old = global_kv[:, 0]
    pseudo = old - summed / replicas
    new_mom = 0.9 * momentum[:, 0] + pseudo
    new_glob = old - 0.7 * (pseudo + 0.9 * new_mom)
    fresh = jnp.concatenate([new_glob[0], new_glob[1]], axis=1).astype(bf16)
    pieces = [fresh] + [
        lax.ppermute(fresh, "fsdp", [(a, (a + d) % n_fsdp) for a in range(n_fsdp)])
        for d in (1, 2, 3)
    ]
    four = jnp.stack([lax.select_n((me - f) & (n_fsdp - 1), *pieces) for f in range(n_fsdp)])
    across = lax.ppermute(four, "worker", move_y())
    block = jnp.stack(
        [jnp.where(upper == 0, four, across), jnp.where(upper == 0, across, four)], axis=1
    )
    group = 2 * n_fsdp
    block = block.reshape(group * shard, 2 * columns)
    running = ring_move([after(r, four) for r in ready])
    late = after(tokens, four)
    ready = ring_terms(1, running, after(tokens, fresh))
    running = ring_move(ready)
    left = lax.ppermute(block, "worker", move_x(1))
    right = lax.ppermute(block, "worker", move_x(3))
    half = group * shard // 2

    def head(chunk):
        found = jnp.einsum("sk,rk->sr", both, chunk, preferred_element_type=f32).astype(bf16)
        low, high = found[:, :half], found[:, half:]
        return jnp.where(side == 0, low, high), jnp.where(side == 0, high, low)

    def spread(chunk):
        other = lax.ppermute(chunk, "worker", move_core())
        pairs = [head(chunk), head(other)]
        return other, [p[0] for p in pairs], [p[1] for p in pairs]

    def project(total, d, mine, other):
        place = (here - d) & 3
        for which, chunk in ((core, mine), (1 - core, other)):
            part = jnp.concatenate(
                [
                    lax.dynamic_slice_in_dim(
                        late, g * 8 * shard + (place * CORES + which) * shard, shard, axis=1
                    )
                    for g in range(group)
                ],
                axis=1,
            )
            more = jnp.dot(part, chunk, preferred_element_type=f32)
            total = more if total is None else total + more
        return total

    def slots(*hops):
        places = [((here - d) & 3) * CORES for d in hops]
        return jnp.stack([s for p in places for s in (p + core, p + 1 - core)])

    swap = [(0, 1), (1, 0)]
    other, kept0, sent = spread(block)
    sent = jnp.stack(sent)
    theirs0 = lax.ppermute(sent, "tensor", swap)
    proj = project(None, 0, block, other)
    left, right = after(left, sent), after(right, sent)
    other_left, kept1, sent_left = spread(left)
    other_right, kept3, sent_right = spread(right)
    sent = jnp.stack(sent_left + sent_right)
    up = lax.ppermute(after(left[:half], theirs0, sent), "worker", move_x(1))
    down = lax.ppermute(after(right[half:], theirs0, sent), "worker", move_x(3))
    theirs1 = lax.ppermute(sent, "tensor", swap)
    ready = ring_terms(2, [after(r, sent) for r in running], late)
    running = ring_move(ready)
    far = jnp.concatenate([up, down], axis=0)
    proj = project(proj, 1, left, other_left)
    proj = project(proj, 3, right, other_right)
    other, kept2, sent = spread(far)
    sent = jnp.stack(sent)
    theirs2 = lax.ppermute(sent, "tensor", swap)
    proj = project(proj, 2, far, other)
    near = after(jnp.stack(kept0), sent)
    dnormed = put(slots(0), near, after(theirs0, sent), None, width // 2)
    near = after(jnp.stack(kept1 + kept3), sent)
    dnormed = put(slots(1, 3), near, after(theirs1, sent), dnormed, width // 2)
    grad = jnp.stack(ring_terms(3, [after(r, dnormed) for r in running], late))
    dnormed = put(slots(2), jnp.stack(kept2), theirs2, dnormed, width // 2)
    keys = rotate(
        proj[:, :columns].reshape(count, heads, HEAD_DIM), pos, 1.0
    ).reshape(count, columns)
    kv_out = jnp.stack([keys, proj[:, columns:]], axis=1).astype(bf16)
    return (new_glob[:, None], new_mom[:, None], kv_out[None], grad[None], dnormed[None])


def solution(mesh):
    placed = (
        P("worker", "fsdp", None),
        P("worker", "fsdp", None, "tensor"),
        P("worker", None, "fsdp", "tensor"),
        P(None, "fsdp", "worker", "tensor"),
        P(None, "fsdp", "worker", "tensor"),
    )
    return jax.shard_map(
        per_device,
        mesh=mesh,
        in_specs=placed,
        out_specs=(
            P(None, "fsdp", "worker", "tensor"),
            P(None, "fsdp", "worker", "tensor"),
            P("worker", "fsdp", None, "tensor"),
            P("worker", None, "fsdp", "tensor"),
            P("worker", "fsdp", "tensor"),
        ),
        check_vma=False,
    )
```

```python
import math

import jax
import jax.numpy as jnp
from jax import lax
from jax.experimental import pallas as pl
from jax.experimental.pallas import tpu as pltpu
from jax.sharding import PartitionSpec as P

HEAD_DIM = 128


def rotate(block, pos, sign):
    half = block.shape[-1] // 2
    index = jnp.arange(half, dtype=jnp.float32)
    freq = jnp.exp(-(2.0 * index / block.shape[-1]) * math.log(500000.0))
    angle = pos[:, None] * freq[None, :]
    cosine = jnp.cos(angle)[:, None, :]
    sine = jnp.sin(angle)[:, None, :]
    first = block[..., :half]
    second = block[..., half:]
    return jnp.concatenate(
        [first * cosine - sign * second * sine, second * cosine + sign * first * sine], axis=-1
    )


def put_kernel(slots, kept, theirs, *rest):
    rest[-1][...] = (kept[0].astype(jnp.float32) + theirs[0].astype(jnp.float32)).astype(
        rest[-1].dtype
    )


def put(slots, kept, theirs, wide, width):
    cores, count, length = kept.shape
    lane = 128
    piece = pl.BlockSpec((1, count, lane), lambda k, g, slots: (k, 0, g))
    earlier = () if wide is None else (wide,)
    return pl.pallas_call(
        put_kernel,
        out_shape=jax.ShapeDtypeStruct((count, width), kept.dtype),
        grid_spec=pltpu.PrefetchScalarGridSpec(
            num_scalar_prefetch=1,
            grid=(cores, length // lane),
            in_specs=[piece, piece] + [pl.BlockSpec(memory_space=pl.ANY)] * len(earlier),
            out_specs=pl.BlockSpec((count, lane), lambda k, g, slots: (0, g * 8 + slots[k])),
        ),
        input_output_aliases={3: 0} if earlier else {},
        cost_estimate=pl.CostEstimate(
            flops=kept.size, bytes_accessed=6 * kept.size, transcendentals=0
        ),
    )(slots, kept, theirs, *earlier)


CORES, ALONG_X = 2, 4


def move_core():
    return [(w, w ^ 1) for w in range(16)]


def move_y():
    return [(w, w ^ 8) for w in range(16)]


def move_x(d):
    return [(w, (w & 9) | ((((w >> 1) + d) & 3) << 1)) for w in range(16)]


def after(value, *earlier):
    return lax.optimization_barrier((value, *earlier))[0]


def take(array, index, axis):
    return lax.dynamic_index_in_dim(array, index, axis, keepdims=False)


def per_device(normed, kv_cotangent, local_kv, global_kv, momentum):
    replicas = lax.axis_size("worker")
    n_fsdp = lax.axis_size("fsdp")
    worker = lax.axis_index("worker")
    core, here, upper = worker & 1, (worker >> 1) & 3, worker >> 3
    me = lax.axis_index("fsdp")
    side = lax.axis_index("tensor")
    tokens = normed[0]
    count, width = tokens.shape
    rows = width // n_fsdp
    columns = local_kv.shape[3]
    heads = columns // HEAD_DIM
    shard = global_kv.shape[2]
    f32, bf16 = jnp.float32, jnp.bfloat16

    local = local_kv[0].reshape(2, 2, ALONG_X, CORES, shard, columns)
    got = lax.ppermute(take(local, 1 - core, 3), "worker", move_core())

    pos = (me * count + jnp.arange(count)).astype(f32)
    cotangent = kv_cotangent[0]
    back = rotate(
        cotangent[:, 0].astype(f32).reshape(count, heads, HEAD_DIM), pos, -1.0
    ).reshape(count, columns)
    raw = (back.astype(bf16), cotangent[:, 1])
    both = jnp.concatenate(raw, axis=1)

    def ring_terms(step, running, tokens):
        ready = []
        for kind, way in ((0, 1), (1, -1)):
            block = (me - way * (step + 1)) & (n_fsdp - 1)
            part = lax.dynamic_slice_in_dim(tokens, block * rows, rows, axis=1)
            mine = jnp.einsum("sr,sc->rc", part, raw[kind], preferred_element_type=f32)
            if step > 0:
                mine = mine + running[kind].astype(f32)
            ready.append(mine.astype(bf16))
        return ready

    def ring_move(ready):
        return [
            lax.ppermute(out, "fsdp", [(a, (a + way) % n_fsdp) for a in range(n_fsdp)])
            for out, way in zip(ready, (1, -1))
        ]

    pair = (take(local, core, 3).astype(f32) + got.astype(f32)).astype(bf16)
    arrived = [
        lax.ppermute(take(pair, (here + d) & 3, 2), "worker", move_x(d)) for d in (1, 3, 2)
    ]
    ready = ring_terms(0, None, after(tokens, pair))
    total = after(take(pair, here, 2), *ready).astype(f32)
    for piece in arrived:
        total = total + piece.astype(f32)
    total = total.astype(bf16)
    got = lax.ppermute(take(total, 1 - upper, 1), "worker", move_y())
    summed = take(total, upper, 1).astype(f32) + got.astype(f32)

    old = global_kv[:, 0]
    pseudo = old - summed / replicas
    new_mom = 0.9 * momentum[:, 0] + pseudo
    new_glob = old - 0.7 * (pseudo + 0.9 * new_mom)
    fresh = jnp.concatenate([new_glob[0], new_glob[1]], axis=1).astype(bf16)
    pieces = [fresh] + [
        lax.ppermute(fresh, "fsdp", [(a, (a + d) % n_fsdp) for a in range(n_fsdp)])
        for d in (1, 2, 3)
    ]
    four = jnp.stack([lax.select_n((me - f) & (n_fsdp - 1), *pieces) for f in range(n_fsdp)])
    across = lax.ppermute(four, "worker", move_y())
    block = jnp.stack(
        [jnp.where(upper == 0, four, across), jnp.where(upper == 0, across, four)], axis=1
    )
    group = 2 * n_fsdp
    block = block.reshape(group * shard, 2 * columns)
    running = ring_move([after(r, four) for r in ready])
    late = after(tokens, four)
    ready = ring_terms(1, running, after(tokens, fresh))
    running = ring_move(ready)
    left = lax.ppermute(block, "worker", move_x(1))
    right = lax.ppermute(block, "worker", move_x(3))
    half = group * shard // 2

    def head(chunk):
        found = jnp.einsum("sk,rk->sr", both, chunk, preferred_element_type=f32).astype(bf16)
        low, high = found[:, :half], found[:, half:]
        return jnp.where(side == 0, low, high), jnp.where(side == 0, high, low)

    def spread(chunk):
        other = lax.ppermute(chunk, "worker", move_core())
        pairs = [head(chunk), head(other)]
        return other, [p[0] for p in pairs], [p[1] for p in pairs]

    def project(total, d, mine, other, late):
        place = (here - d) & 3
        for which, chunk in ((core, mine), (1 - core, other)):
            part = jnp.concatenate(
                [
                    lax.dynamic_slice_in_dim(
                        late, g * 8 * shard + (place * CORES + which) * shard, shard, axis=1
                    )
                    for g in range(group)
                ],
                axis=1,
            )
            more = jnp.dot(part, chunk, preferred_element_type=f32)
            total = more if total is None else total + more
        return total

    def slots(*hops):
        places = [((here - d) & 3) * CORES for d in hops]
        return jnp.stack([s for p in places for s in (p + core, p + 1 - core)])

    swap = [(0, 1), (1, 0)]
    other, kept0, sent = spread(block)
    sent = jnp.stack(sent)
    theirs0 = lax.ppermute(sent, "tensor", swap)
    proj = project(None, 0, block, other, late)
    left, right = after(left, sent), after(right, sent)
    other_left, kept1, sent_left = spread(left)
    other_right, kept3, sent_right = spread(right)
    sent = jnp.stack(sent_left + sent_right)
    up = lax.ppermute(after(left[:half], sent), "worker", move_x(1))
    down = lax.ppermute(after(right[half:], sent), "worker", move_x(3))
    theirs1 = lax.ppermute(sent, "tensor", swap)
    near = after(jnp.stack(kept0), sent)
    dnormed = put(slots(0), near, after(theirs0, sent), None, width // 2)
    ready = ring_terms(2, [after(r, sent) for r in running], late)
    running = ring_move(ready)
    far = jnp.concatenate([up, down], axis=0)
    proj = project(proj, 1, left, other_left, late)
    proj = project(proj, 3, right, other_right, late)
    other, kept2, sent = spread(far)
    sent = jnp.stack(sent)
    theirs2 = lax.ppermute(sent, "tensor", swap)
    proj = project(proj, 2, far, other, after(late, sent))
    near = after(jnp.stack(kept1 + kept3), sent)
    dnormed = put(slots(1, 3), near, after(theirs1, sent), dnormed, width // 2)
    grad = jnp.stack(ring_terms(3, [after(r, dnormed) for r in running], late))
    dnormed = put(slots(2), jnp.stack(kept2), theirs2, dnormed, width // 2)
    keys = rotate(
        proj[:, :columns].reshape(count, heads, HEAD_DIM), pos, 1.0
    ).reshape(count, columns)
    kv_out = jnp.stack([keys, proj[:, columns:]], axis=1).astype(bf16)
    return (new_glob[:, None], new_mom[:, None], kv_out[None], grad[None], dnormed[None])


def solution(mesh):
    placed = (
        P("worker", "fsdp", None),
        P("worker", "fsdp", None, "tensor"),
        P("worker", None, "fsdp", "tensor"),
        P(None, "fsdp", "worker", "tensor"),
        P(None, "fsdp", "worker", "tensor"),
    )
    return jax.shard_map(
        per_device,
        mesh=mesh,
        in_specs=placed,
        out_specs=(
            P(None, "fsdp", "worker", "tensor"),
            P(None, "fsdp", "worker", "tensor"),
            P("worker", "fsdp", None, "tensor"),
            P("worker", None, "fsdp", "tensor"),
            P("worker", "fsdp", "tensor"),
        ),
        check_vma=False,
    )
```
